32 devices in a mesh: dp: 8 (over y, x, core), tensor: 4 (over z).
Axes of the slice: x: 2, y: 2, z: 4, core: 2. Of those that a mesh axis runs over, the one named last changes fastest.
Arguments:
- x_in: bfloat16 [16384, 1024], P(('dp', 'tensor')), may hold values from -6 to 6
- in_w: bfloat16 [1024, 3, 1024], P('dp', None, 'tensor'), may hold values from -0.1875 to 0.1875
- out_w: bfloat16 [1024, 1024], P('tensor', 'dp'), may hold values from -0.1875 to 0.1875
- gate_w: bfloat16 [1024, 4608], P('dp', 'tensor'), may hold values from -0.1875 to 0.1875
- up_w: bfloat16 [1024, 4608], P('dp', 'tensor'), may hold values from -0.1875 to 0.1875
- down_w: bfloat16 [4608, 1024], P('tensor', 'dp'), may hold values from -0.125 to 0.125
- conv_w: bfloat16 [3, 1024], replicated, may hold values from -3 to 3
- gain1: bfloat16 [1024], replicated, may hold values from 0.25 to 1.75
- gain2: bfloat16 [1024], replicated, may hold values from 0.25 to 1.75
- d_out: bfloat16 [16384, 1024], P(('dp', 'tensor')), may hold values from -6 to 6
Outputs:
- block_out: bfloat16 [16384, 1024], P(('dp', 'tensor'))
- d_x: bfloat16 [16384, 1024], P(('dp', 'tensor'))
- grad_in: float32 [1024, 3, 1024], P('dp', None, 'tensor')
- grad_out: float32 [1024, 1024], P('tensor', 'dp')
- grad_gate: float32 [1024, 4608], P('dp', 'tensor')
- grad_up: float32 [1024, 4608], P('dp', 'tensor')
- grad_down: float32 [4608, 1024], P('tensor', 'dp')
- grad_conv: float32 [3, 1024], replicated
- grad_gain1: float32 [1024], replicated
- grad_gain2: float32 [1024], replicated
The draws below stay inside these ranges and needn't reach their ends.
All inputs are finite; a program needn't handle non-finite values.
Results may differ from the reference program's by a relative error of at most 0.018.
Values may be sent and summed in bfloat16 or wider, within the bound.
No kernel may reach another device: no remote copies, remote signals or barrier semaphores. Data moves between devices by JAX's collectives and lax.ppermute only.
A program may use at most 192 MiB of HBM per device.

```python
import jax
import jax.numpy as jnp
from jax import lax

D = 1024
FF = 4608
CONV_LEN = 3
LEN = 1024
TOKENS = 16384


def steps_of(stream_key, extent, split, least, largest):
    loudness = 1.0
    for dim, blocks in split:
        heights = jax.random.uniform(jax.random.fold_in(jax.random.fold_in(stream_key, 6), dim), (blocks,), jnp.float32, least / len(split), largest / len(split))
        loudness = loudness * jnp.repeat(jnp.exp(heights), extent[dim] // blocks).reshape((-1,) + (1,) * (len(extent) - 1 - dim))
    return loudness


def gaussian(stream_key, dims, scale, bound, cuts=(), held_as=jnp.bfloat16):
    factor_of = steps_of(stream_key, dims, cuts, -0.22, 0.18) if cuts else 1.0
    entries = jax.random.normal(stream_key, dims, jnp.float32) * scale * factor_of
    return jnp.minimum(jnp.maximum(entries, -bound), bound).astype(held_as)


def setup_inputs(seed: int = 0) -> dict:
    keys = jax.random.split(jax.random.key(seed), 11)
    return {
        "x_in": gaussian(keys[0], (TOKENS, D), 1.0, 6.0, ((0, 32),)),
        "in_w": gaussian(keys[1], (D, 3, D), D ** -0.5, 0.1875, ((0, 8), (2, 4))),
        "out_w": gaussian(keys[2], (D, D), D ** -0.5, 0.1875, ((0, 4), (1, 8))),
        "gate_w": gaussian(keys[3], (D, FF), D ** -0.5, 0.1875, ((0, 8), (1, 4))),
        "up_w": gaussian(keys[4], (D, FF), D ** -0.5, 0.1875, ((0, 8), (1, 4))),
        "down_w": gaussian(keys[5], (FF, D), (FF // 2) ** -0.5, 0.125, ((0, 4), (1, 8))),
        "conv_w": gaussian(keys[6], (CONV_LEN, D), 0.6, 3.0),
        "gain1": jnp.clip(1.0 + 0.15 * jax.random.normal(keys[7], (D,), jnp.float32), 0.25, 1.75).astype(jnp.bfloat16),
        "gain2": jnp.clip(1.0 + 0.15 * jax.random.normal(keys[8], (D,), jnp.float32), 0.25, 1.75).astype(jnp.bfloat16),
        "d_out": gaussian(keys[9], (TOKENS, D), 1.0, 6.0, ((0, 32),)),
    }


@jax.custom_vjp
def low(v):
    return lax.optimization_barrier(v.astype(jnp.bfloat16)).astype(jnp.float32)

@jax.custom_vjp
def low_back(v):
    return v

def low_keep(v):
    return (low(v), None)

def low_pass(kept, grad):
    return (grad,)

def back_keep(v):
    return (v, None)

def back_low(kept, grad):
    return (low(grad),)
low.defvjp(low_keep, low_pass)
low_back.defvjp(back_keep, back_low)
epsilon = 1e-05
highest = lax.Precision.HIGHEST

def rms_norm(values, gain):
    scale = lax.rsqrt(lax.optimization_barrier(jnp.mean(values * values, axis=-1, keepdims=True)) + epsilon)
    return values * scale * gain

def delayed(values, steps_back):
    zeros = jnp.zeros((steps_back, values.shape[1]), jnp.float32)
    return jnp.concatenate([zeros, values[:values.shape[0] - steps_back]], axis=0)

def block(tokens, in_w, out_w, gate_w, up_w, down_w, conv_w, gain1, gain2):
    first = low(rms_norm(tokens, gain1))
    projected = low_back(jnp.einsum('td,dkc->tkc', first, in_w, precision=highest))
    b_part = projected[:, 0]
    c_part = projected[:, 1]
    x_part = projected[:, 2]
    mixed_in = b_part * x_part
    conv_out = conv_w[2] * mixed_in + conv_w[1] * delayed(mixed_in, 1) + conv_w[0] * delayed(mixed_in, 2)
    branch = low(c_part * conv_out)
    mixed = low_back(jnp.dot(branch, out_w, precision=highest))
    resid = tokens + mixed
    second = low(rms_norm(resid, gain2))
    gate = low_back(jnp.dot(second, gate_w, precision=highest))
    up_val = low_back(jnp.dot(second, up_w, precision=highest))
    hidden = low(jax.nn.silu(gate) * up_val)
    ffn = low_back(jnp.dot(hidden, down_w, precision=highest))
    return resid + ffn

def reference(x_in, in_w, out_w, gate_w, up_w, down_w, conv_w, gain1, gain2, d_out):
    params = tuple((p.astype(jnp.float32) for p in (in_w, out_w, gate_w, up_w, down_w, conv_w, gain1, gain2)))
    sequences = x_in.astype(jnp.float32).reshape(-1, LEN, D)
    cotangents = d_out.astype(jnp.float32).reshape(-1, LEN, D)

    def one_sequence(totals, pair):
        tokens, cotangent = pair
        result, pull = jax.vjp(block, tokens, *params)
        grads = pull(cotangent)
        totals = tuple((a + b for a, b in zip(totals, grads[1:])))
        return (totals, (result, grads[0]))
    start = tuple((jnp.zeros_like(p) for p in params))
    totals, (results, input_grads) = lax.scan(one_sequence, start, (sequences, cotangents))
    block_out = results.reshape(-1, D).astype(jnp.bfloat16)
    d_x = input_grads.reshape(-1, D).astype(jnp.bfloat16)
    return (block_out, d_x, totals[0], totals[1], totals[2], totals[3], totals[4], totals[5], totals[6], totals[7])
```

```python
import jax
import jax.numpy as jnp
import numpy as np
from jax import lax
from jax.sharding import PartitionSpec as P

LEN = 1024
epsilon = 1e-05
AXES = ("dp", "tensor")
bf16 = jnp.bfloat16
f32 = jnp.float32


class Links:
    def __init__(self, dp, tensor):
        self.dp, self.tensor = dp, tensor
        self.bits = (dp // 2).bit_length() - 1
        assert dp == 2 << self.bits
        self.devices = [(d, t) for d in range(dp) for t in range(tensor)]

    def at(self, d, t):
        return d * self.tensor + t

    def pairs(self, target):
        return [(self.at(d, t), self.at(*target(d, t))) for d, t in self.devices]

    def shift(self, k):
        return self.pairs(lambda d, t: (d, (t - k) % self.tensor))

    def flip(self, core, step):
        return 2 << (step if core == 0 else self.bits - 1 - step)

    def step(self, j):
        return self.pairs(lambda d, t: (d ^ self.flip(d % 2, j), t))

    def cores(self):
        return self.pairs(lambda d, t: (d ^ 1, t))

    def order(self):
        table = np.zeros((self.dp, self.dp), np.int32)
        half = self.dp // 2
        for d in range(self.dp):
            for p in range(self.dp):
                source = d ^ 1 if p >= half else d
                for j in range(self.bits):
                    if (p >> j) & 1:
                        source ^= self.flip(source % 2, j)
                table[d, p] = source
        return table


def send(x, pairs):
    return lax.ppermute(x, AXES, pairs)


def gather(links, x, order):
    step = 0
    for name in order:
        if name == "z":
            x = jnp.concatenate([x] + [send(x, links.shift(k)) for k in range(1, links.tensor)], axis=1)
        else:
            x = jnp.concatenate([x, send(x, links.step(step))], axis=0)
            step += 1
    return x, send(x, links.cores())


def scatter_sum(links, own, other):
    x = own.astype(f32) + send(other, links.cores()).astype(f32)
    for j in reversed(range(links.bits)):
        half = x.shape[0] // 2
        away = x[half:].astype(bf16)
        x = x[:half] + send(away, links.step(j)).astype(f32)
    n = x.shape[1] // links.tensor
    total = x[:, :n]
    for k in range(1, links.tensor):
        back = [(b, a) for a, b in links.shift(k)]
        total = total + send(x[:, k * n : (k + 1) * n].astype(bf16), back).astype(f32)
    return total


def sum_all(links, x):
    x = x + send(x, links.cores())
    for j in range(links.bits):
        x = x + send(x, links.step(j))
    k = 1
    while k < links.tensor:
        x = x + send(x, links.pairs(lambda d, t: (d, t ^ k)))
        k *= 2
    return x


def dot(a, b, ca, cb):
    return lax.dot_general(a, b, (((ca,), (cb,)), ((), ())), preferred_element_type=f32)


def norm_rows(values):
    scale = lax.rsqrt(jnp.mean(values * values, axis=-1, keepdims=True) + epsilon)
    return (values * scale, scale)


def norm_back(grad_h, normed, scale, gain):
    grad_n = grad_h * gain
    inner = jnp.mean(grad_n * normed, axis=-1, keepdims=True)
    return scale * (grad_n - normed * inner)


def make_body(links):
    dp, T = links.dp, links.tensor
    table = links.order()

    def body(x_in, in_w, out_w, gate_w, up_w, down_w, conv_w, gain1, gain2, d_out):
        rows, D = x_in.shape
        block = D // dp
        half = D // 2
        chan = in_w.shape[2]
        C = chan * T
        FF = gate_w.shape[1] * T
        per_seq = LEN // rows
        me_dp = lax.axis_index("dp")
        me_t = lax.axis_index("tensor")

        conv_blocks = jnp.concatenate([in_w.reshape(block, 3 * chan), out_w.T], axis=1)
        stages = ["x"] * links.bits
        conv0, conv1 = gather(links, conv_blocks, ["z"] + stages)
        gate0, gate1 = gather(links, gate_w, ["z"] + stages)
        up0, up1 = gather(links, up_w, ["z"] + stages)
        down0, down1 = gather(links, down_w.T, ["z"] + stages)

        def split_conv(w):
            w = w.reshape(half, T, 4, chan)
            return [w[:, :, k].reshape(half, C) for k in range(4)]

        b0, c0, x0, out0 = split_conv(conv0)
        b1, c1, x1, out1 = split_conv(conv1)

        mine = jnp.take(jnp.asarray(table), me_dp, axis=0)
        source = (mine[:, None] * block + jnp.arange(block)[None, :]).reshape(D)
        place = (jnp.arange(D)[:, None] == source[None, :]).astype(bf16)

        def arrange(v):
            return dot(v, place, 1, 0).astype(bf16)

        def restore(v):
            return dot(v, place, 1, 1).astype(bf16)

        def restore_rows(v):
            return jnp.sum(
                jnp.where((mine[None, :] == jnp.arange(dp)[:, None])[:, :, None], v.reshape(1, dp, block), 0.0), axis=1
            ).reshape(D)

        tokens = arrange(x_in).astype(f32)
        cot16 = arrange(d_out)
        gains = arrange(jnp.stack([gain1, gain2])).astype(f32)
        gain_one, gain_two = gains[0], gains[1]
        turned = jnp.concatenate([conv_w, conv_w], axis=1)
        kernel = lax.dynamic_slice_in_dim(turned, me_t * chan, C, 1).astype(f32)

        normed_one, scale_one = norm_rows(tokens)
        first = (normed_one * gain_one).astype(bf16)

        def proj(a, w0, w1):
            return dot(a[:, :half], w0, 1, 0) + dot(a[:, half:], w1, 1, 0)

        def proj_t(a, w0, w1):
            return jnp.concatenate([dot(a, w0, 1, 1), dot(a, w1, 1, 1)], axis=1)

        b_part = proj(first, b0, b1)
        c_part = proj(first, c0, c1)
        x_part = proj(first, x0, x1)
        mixed_in = b_part * x_part
        follows = [(links.at(d, t), links.at(d, t + 1)) for d, t in links.devices if (t + 1) % per_seq]
        before = send(jnp.roll(mixed_in[rows - 2 :], -chan, axis=1), follows) if follows else jnp.zeros((2, C), f32)
        lead = jnp.concatenate([before, mixed_in[: rows - 1]], axis=0)
        back_one = lead[1:]
        back_two = lead[:rows]
        conv_out = kernel[2] * mixed_in + kernel[1] * back_one + kernel[0] * back_two
        branch = (c_part * conv_out).astype(bf16)
        resid = tokens + proj_t(branch, out0, out1)
        normed_two, scale_two = norm_rows(resid)
        second = (normed_two * gain_two).astype(bf16)
        gate = proj(second, gate0, gate1)
        up_val = proj(second, up0, up1)
        sigma = jax.nn.sigmoid(gate)
        silu_gate = gate * sigma
        hidden = (silu_gate * up_val).astype(bf16)

        def weight_grad(a, b):
            return dot(a[:, :half], b, 0, 0).astype(bf16), dot(a[:, half:], b, 0, 0).astype(bf16)

        grad_down = scatter_sum(links, *weight_grad(cot16, hidden)).T
        d_hidden = proj(cot16, down0, down1)
        d_gate = (d_hidden * up_val * sigma * (1.0 + gate * (1.0 - sigma))).astype(bf16)
        d_up = (d_hidden * silu_gate).astype(bf16)
        grad_gate = scatter_sum(links, *weight_grad(second, d_gate))
        grad_up = scatter_sum(links, *weight_grad(second, d_up))
        d_second = proj_t(d_gate, gate0, gate1) + proj_t(d_up, up0, up1)
        gain_two_part = jnp.sum(d_second * normed_two, axis=0)
        d_resid = cot16.astype(f32) + norm_back(d_second, normed_two, scale_two, gain_two)
        d_mixed = d_resid.astype(bf16)
        d_branch = proj(d_mixed, out0, out1)
        grad_out = scatter_sum(links, *weight_grad(d_mixed, branch)).T
        d_conv = d_branch * c_part
        d_c = d_branch * conv_out
        leads = [(b, a) for a, b in follows]
        after = send(jnp.roll(d_conv[:2], chan, axis=1), leads) if leads else jnp.zeros((2, C), f32)
        trail = jnp.concatenate([d_conv[1:], after], axis=0)
        d_mixin = kernel[2] * d_conv + kernel[1] * trail[:rows] + kernel[0] * trail[1:]
        taps = [jnp.sum(d_conv * v, axis=0) for v in (back_two, back_one, mixed_in)]
        d_b = (d_mixin * x_part).astype(bf16)
        d_c = d_c.astype(bf16)
        d_xpart = (d_mixin * b_part).astype(bf16)
        grads_in = [scatter_sum(links, *weight_grad(first, v)) for v in (d_b, d_c, d_xpart)]
        grad_in = jnp.stack(grads_in, axis=1)
        d_first = proj_t(d_b, b0, b1) + proj_t(d_c, c0, c1) + proj_t(d_xpart, x0, x1)
        gain_one_part = jnp.sum(d_first * normed_one, axis=0)
        d_x = restore((d_resid + norm_back(d_first, normed_one, scale_one, gain_one)).astype(bf16))
        block_out = restore((resid + proj_t(hidden, down0, down1)).astype(bf16))

        taps = jnp.stack(taps)
        taps = lax.dynamic_slice_in_dim(jnp.concatenate([taps, taps], axis=1), C - me_t * chan, C, 1)
        small = jnp.concatenate([taps, restore_rows(gain_one_part)[None], restore_rows(gain_two_part)[None]], axis=0)
        small = sum_all(links, small)
        return (
            block_out,
            d_x,
            grad_in,
            grad_out,
            grad_gate,
            grad_up,
            grad_down,
            small[:3],
            small[3],
            small[4],
        )

    return body


def solution(mesh):
    links = Links(mesh.shape["dp"], mesh.shape["tensor"])
    in_specs = (
        P(("dp", "tensor"), None),
        P("dp", None, "tensor"),
        P("tensor", "dp"),
        P("dp", "tensor"),
        P("dp", "tensor"),
        P("tensor", "dp"),
        P(),
        P(),
        P(),
        P(("dp", "tensor"), None),
    )
    out_specs = (
        P(("dp", "tensor"), None),
        P(("dp", "tensor"), None),
        P("dp", None, "tensor"),
        P("tensor", "dp"),
        P("dp", "tensor"),
        P("dp", "tensor"),
        P("tensor", "dp"),
        P(),
        P(),
        P(),
    )
    return jax.shard_map(
        make_body(links), mesh=mesh, in_specs=in_specs, out_specs=out_specs, check_vma=False
    )
```

```python
import jax
import jax.numpy as jnp
from jax import lax
from jax.experimental import pallas as pl
from jax.experimental.pallas import tpu as pltpu
from jax.sharding import PartitionSpec as P

LEN = 1024
epsilon = 1e-05
AXES = ("dp", "tensor")
bf16 = jnp.bfloat16
f32 = jnp.float32
TOKEN_BLOCK = 512
INTERPRET = False


class Links:
    def __init__(self, dp, tensor):
        self.dp, self.tensor = dp, tensor
        self.bits = (dp // 2).bit_length() - 1
        assert dp == 2 << self.bits and self.bits >= 1
        self.devices = [(d, t) for d in range(dp) for t in range(tensor)]

    def at(self, d, t):
        return d * self.tensor + t

    def pairs(self, target):
        return [(self.at(d, t), self.at(*target(d, t))) for d, t in self.devices]

    def shift(self, k):
        return self.pairs(lambda d, t: (d, (t - k) % self.tensor))

    def bit(self, core, step):
        return step if core == 0 else self.bits - 1 - step

    def step(self, j):
        return self.pairs(lambda d, t: (d ^ (2 << self.bit(d % 2, j)), t))

    def flip(self, j):
        return self.pairs(lambda d, t: (d ^ (2 << j), t))

    def cores(self):
        return self.pairs(lambda d, t: (d ^ 1, t))

    def spread(self, p):
        return ((p << 1) | (p >> self.bits)) & (self.dp - 1)


def send(x, pairs):
    return lax.ppermute(x, AXES, pairs)


def dot(a, b, ca, cb):
    return lax.dot_general(a, b, (((ca,), (cb,)), ((), ())), preferred_element_type=f32)


def norm_rows(values):
    scale = lax.rsqrt(jnp.mean(values * values, axis=-1, keepdims=True) + epsilon)
    return (values * scale, scale)


def norm_back(grad_h, normed, scale, gain):
    grad_n = grad_h * gain
    inner = jnp.mean(grad_n * normed, axis=-1, keepdims=True)
    return scale * (grad_n - normed * inner)


def after(x, *others):
    return lax.optimization_barrier((x,) + others)[0]


def ffn_kernel(first_call, part, *refs):
    if first_call:
        h_ref, g_ref, *w_refs, dh_ref, ffn_ref, own0_ref, own1_ref, other_ref, acc_ref = refs
        dh_sum, ffn_sum = None, None
    else:
        h_ref, g_ref, *w_refs, dh_sum, ffn_sum, dh_ref, ffn_ref, own0_ref, own1_ref, other_ref, acc_ref = refs
    step = pl.program_id(0)
    both = 2 * part
    q = w_refs[0].shape[1]
    h, g = h_ref[...], g_ref[...]
    cut = [slice(i * q, (i + 1) * q) for i in range(4)]
    gate_up = sum(dot(w[:both], h[:, c], 1, 1) for w, c in zip(w_refs, cut))
    d_hidden = sum(dot(w[both:], g[:, c], 1, 1) for w, c in zip(w_refs, cut))
    gate, up = gate_up[:part], gate_up[part:]
    sigma = 1.0 / (1.0 + jnp.exp(-gate))
    silu = gate * sigma
    hidden = (silu * up).astype(bf16)
    d_gate = (d_hidden * up * sigma * (1.0 + gate * (1.0 - sigma))).astype(bf16)
    d_up = (d_hidden * silu).astype(bf16)
    d_both = jnp.concatenate([d_gate, d_up], axis=0)
    for w, c in zip(w_refs, cut):
        d_h = dot(d_both, w[:both], 0, 0)
        ffn = dot(hidden, w[both:], 0, 0)
        dh_ref[:, c] = d_h if first_call else dh_sum[:, c] + d_h
        ffn_ref[:, c] = ffn if first_call else ffn_sum[:, c] + ffn

    @pl.when(step == 0)
    def _():
        acc_ref[:both] = dot(d_both, h, 1, 0)
        acc_ref[both:] = dot(hidden, g, 1, 0)

    @pl.when(step > 0)
    def _():
        acc_ref[:both] += dot(d_both, h, 1, 0)
        acc_ref[both:] += dot(hidden, g, 1, 0)

    @pl.when(step == pl.num_programs(0) - 1)
    def _():
        own0_ref[...] = acc_ref[:, cut[0]].astype(bf16)
        own1_ref[...] = acc_ref[:, cut[1]].astype(bf16)
        other_ref[...] = acc_ref[:, 2 * q :].astype(bf16)


def ffn_chunk(h, g, weights, totals, token_block):
    tokens, D = h.shape
    n, q = weights[0].shape
    part = n // 3
    first_call = totals is None
    by_tokens = pl.BlockSpec((token_block, D), lambda i: (i, 0))
    whole = lambda w: pl.BlockSpec((n, w), lambda i: (0, 0))
    args = [h, g, *weights] + ([] if first_call else list(totals))
    specs = [by_tokens, by_tokens] + [whole(q)] * 4 + ([] if first_call else [by_tokens] * 2)

    def kernel(*refs):
        ffn_kernel(first_call, part, *refs)

    return pl.pallas_call(
        kernel,
        grid=(tokens // token_block,),
        in_specs=specs,
        out_specs=[
            by_tokens,
            by_tokens,
            whole(q),
            whole(q),
            whole(2 * q),
        ],
        out_shape=[
            jax.ShapeDtypeStruct((tokens, D), f32),
            jax.ShapeDtypeStruct((tokens, D), f32),
            jax.ShapeDtypeStruct((n, q), bf16),
            jax.ShapeDtypeStruct((n, q), bf16),
            jax.ShapeDtypeStruct((n, 2 * q), bf16),
        ],
        scratch_shapes=[pltpu.VMEM((n, D), f32)],
        compiler_params=pltpu.CompilerParams(
            dimension_semantics=("arbitrary",), vmem_limit_bytes=52 * 1024 * 1024
        ),
        cost_estimate=pl.CostEstimate(
            flops=20 * tokens * D * part, bytes_accessed=12 * n * q * 2, transcendentals=tokens * part
        ),
        interpret=INTERPRET,
    )(*args)


def make_body(links):
    dp, T = links.dp, links.tensor

    def body(x_in, in_w, out_w, gate_w, up_w, down_w, conv_w, gain1, gain2, d_out):
        rows, D = x_in.shape
        block = D // dp
        half = D // 2
        chan = in_w.shape[2]
        C = chan * T
        part = gate_w.shape[1] // 2
        per_seq = LEN // rows
        me_dp = lax.axis_index("dp")
        me_t = lax.axis_index("tensor")
        me_x = (me_dp // 2) % 2
        core = me_dp % 2
        groups = dp // 2
        canonical = [
            [sum(((q >> links.bit(c, j)) & 1) << j for j in range(links.bits)) for q in range(groups)] for c in (0, 1)
        ]
        walked = [[order.index(p) for p in range(groups)] for order in canonical]

        def by_core(blocks, order):
            a, b = order
            return [blocks[i] if i == j else jnp.where(core == 0, blocks[i], blocks[j]) for i, j in zip(a, b)]

        def walk_back(own, got):
            x = own.astype(f32) + got.astype(f32)
            blocks = by_core([x[i * block : (i + 1) * block] for i in range(groups)], walked)
            for j in reversed(range(links.bits)):
                n = len(blocks) // 2
                sent = send(jnp.concatenate(blocks[n:], axis=0).astype(bf16), links.step(j)).astype(f32)
                blocks = [blocks[i] + sent[i * block : (i + 1) * block] for i in range(n)]
            return blocks[0]

        def shift_back(k, x):
            return send(x.astype(bf16), [(b, a) for a, b in links.shift(k)])

        def swap(v):
            parts = [v[:, (p ^ 1) * block : ((p ^ 1) + 1) * block] for p in range(dp)]
            return jnp.concatenate(parts, axis=1)

        mine = me_dp ^ jnp.asarray([links.spread(p) for p in range(dp)], jnp.int32)
        source = (mine[:, None] * block + jnp.arange(block)[None, :]).reshape(D)
        place = (jnp.arange(D)[:, None] == source[None, :]).astype(bf16)

        def arrange(v):
            return dot(v, place, 1, 0).astype(bf16)

        def restore(v):
            return dot(v, place, 1, 1).astype(bf16)

        def restore_rows(v):
            return jnp.sum(
                jnp.where((mine[None, :] == jnp.arange(dp)[:, None])[:, :, None], v.reshape(1, dp, block), 0.0), axis=1
            ).reshape(D)

        in_own = in_w.reshape(block, 3 * chan)
        in_k = [in_own] + [send(in_own, links.shift(k)) for k in range(1, T)]
        stack = jnp.concatenate([w.reshape(2, part, block) for w in (gate_w.T, up_w.T, down_w)], axis=1)
        ffn_keep = jnp.where(me_x == 0, stack[0], stack[1])
        ffn_give = jnp.where(me_x == 0, stack[1], stack[0])
        ffn_own = jnp.concatenate([ffn_keep, send(ffn_give, links.flip(0))], axis=1)

        own = [ffn_own]
        near = [[] for _ in range(T)]

        def shift_chunk(*waits):
            if len(own) < T:
                own.append(send(after(own[-1], *waits), links.shift(1)))

        def exchange(k, *waits):
            if k < T:
                x = after(own[k], *waits)
                for j in range(1, links.bits):
                    got = send(x, links.flip(j))
                    near[k] = [x, got]
                    if j < links.bits - 1:
                        x = jnp.concatenate(near[k], axis=1)

        def walk_first(x):
            return [x, send(x, links.step(0))]

        def walk_rest(blocks, *waits):
            for j in range(1, links.bits):
                whole = jnp.concatenate(blocks, axis=0)
                if j == 1:
                    whole = after(whole, *waits)
                got = send(whole, links.step(j))
                blocks = blocks + [got[i * block : (i + 1) * block] for i in range(len(blocks))]
            return blocks

        in_cols = jnp.concatenate([w[:, i * chan : (i + 1) * chan] for i in range(3) for w in in_k], axis=1)
        in_cols = after(in_cols, ffn_own)
        in_first = walk_first(in_cols)
        out_own = after(out_w.T, in_cols)
        out_k = [out_own] + [send(out_own, links.shift(k)) for k in range(1, T)]
        out_cols = jnp.concatenate(out_k, axis=1)
        slot2 = [in_first[1], out_cols]
        in_walked = walk_rest(in_first, *slot2)
        out_first = walk_first(after(out_cols, *slot2))
        shift_chunk(*slot2)
        slot3 = [in_walked[-1], own[-1], out_first[1]]
        in0 = after(jnp.concatenate(by_core(in_walked, canonical), axis=0), *slot3)
        in1 = send(in0, links.cores())
        out_walked = walk_rest(out_first, *slot3)
        shift_chunk(*slot3)
        exchange(1, *slot3)
        out0 = jnp.concatenate(by_core(out_walked, canonical), axis=0)
        out1 = send(out0, links.cores())

        tokens = arrange(x_in).astype(f32)
        cot16 = arrange(d_out)
        partner_cot = send(after(swap(cot16), *slot3), links.flip(0))
        gains = arrange(jnp.stack([gain1, gain2])).astype(f32)
        gain_one, gain_two = gains[0], gains[1]
        turned = jnp.concatenate([conv_w, conv_w], axis=1)
        kernel = lax.dynamic_slice_in_dim(turned, me_t * chan, C, 1).astype(f32)

        def split(a, axis=1):
            return lax.slice_in_dim(a, 0, half, axis=axis), lax.slice_in_dim(a, half, D, axis=axis)

        normed_one, scale_one = norm_rows(tokens)
        first = (normed_one * gain_one).astype(bf16)
        f0, f1 = split(first)
        projected = dot(f0, in0, 1, 0) + dot(f1, in1, 1, 0)
        b_part, c_part, x_part = projected[:, :C], projected[:, C : 2 * C], projected[:, 2 * C :]
        mixed_in = b_part * x_part
        follows = [(links.at(d, t), links.at(d, t + 1)) for d, t in links.devices if (t + 1) % per_seq]
        no_rows = jnp.zeros((2, C), f32)
        before = send(jnp.roll(mixed_in[rows - 2 :], -chan, axis=1), follows) if follows else no_rows
        lead = jnp.concatenate([before, mixed_in[: rows - 1]], axis=0)
        back_one = lead[1:]
        back_two = lead[:rows]
        conv_out = kernel[2] * mixed_in + kernel[1] * back_one + kernel[0] * back_two
        branch = (c_part * conv_out).astype(bf16)
        slot4 = [out_walked[-1], own[-1], partner_cot] + near[1 % T]
        branch = after(branch, *slot4)
        exchange(2, branch)
        shift_chunk(branch)
        resid = tokens + jnp.concatenate([dot(branch, out0, 1, 1), dot(branch, out1, 1, 1)], axis=1)
        normed_two, scale_two = norm_rows(resid)
        second = (normed_two * gain_two).astype(bf16)
        cot_all = jnp.concatenate([partner_cot, cot16], axis=0)
        second_all = jnp.concatenate([send(swap(second), links.flip(0)), second], axis=0)

        def core_sum(k, sums):
            own0, own1, other = sums
            got = send(other, links.cores()).astype(f32)
            return own0.astype(f32) + got[:, : half // 2], (own1.astype(f32) + got[:, half // 2 :]).astype(bf16)

        def group_sum(kept, sent):
            x = kept + send(sent, links.flip(links.bits - 1)).astype(f32)
            for j in reversed(range(1, links.bits - 1)):
                n = x.shape[1] // 2
                x = x[:, :n] + send(x[:, n:].astype(bf16), links.flip(j)).astype(f32)
            return x

        def other_core(k):
            return near[k] + [send(x, links.cores()) for x in near[k]]

        turn = list(range(1, T)) + [0]
        totals = None
        sums, cored, grouped, shifted = {}, {}, {}, {}
        weights = {}
        if T == 1:
            exchange(0)
        weights[turn[0]] = other_core(turn[0])
        slot = weights[turn[0]] + [x for k in turn[:2] for x in near[k]] + own
        for i, k in enumerate(turn):
            h_in = after(second_all, *slot)
            slot = []
            if i + 2 < T:
                exchange(turn[i + 2], h_in)
                slot += near[turn[i + 2]]
            if i + 1 < T:
                weights[turn[i + 1]] = other_core(turn[i + 1])
                slot += weights[turn[i + 1]]
            if i >= 1:
                cored[i - 1] = core_sum(turn[i - 1], sums[i - 1])
                slot += cored[i - 1]
            if i >= 2:
                grouped[i - 2] = group_sum(*cored[i - 2])
                slot.append(grouped[i - 2])
            if i >= 3:
                shifted[i - 3] = shift_back(turn[i - 3], grouped[i - 3])
                slot.append(shifted[i - 3])
            d_h, ffn, *sums[i] = ffn_chunk(h_in, cot_all, weights[k], totals, min(TOKEN_BLOCK, 2 * rows))
            totals = (d_h, ffn)

        theirs = send(swap(d_h[:rows].astype(bf16)), links.flip(0))
        ready = after(d_h[:8], *slot)
        cored[T - 1] = core_sum(turn[T - 1], sums[T - 1])
        if T > 1:
            grouped[T - 2] = group_sum(cored[T - 2][0], after(cored[T - 2][1], ready))
        if T > 2:
            shifted[T - 3] = shift_back(turn[T - 3], after(grouped[T - 3], ready))
        theirs = after(theirs, *cored[T - 1], ready)
        d_second = d_h[rows:] + theirs.astype(f32)
        ffn_sent = send(after(swap(ffn[:rows].astype(bf16)), theirs), links.flip(0))
        ffn_theirs = ffn_sent.astype(f32)

        gain_two_part = jnp.sum(d_second * normed_two, axis=0)
        d_resid = cot16.astype(f32) + norm_back(d_second, normed_two, scale_two, gain_two)
        d_mixed = d_resid.astype(bf16)
        m0, m1 = split(d_mixed)
        d_branch = dot(m0, out0, 1, 0) + dot(m1, out1, 1, 0)
        d_conv = d_branch * c_part
        d_c = d_branch * conv_out
        leads = [(b, a) for a, b in follows]
        edge = send(jnp.roll(d_conv[:2], chan, axis=1), leads) if leads else no_rows
        d_c = d_c.astype(bf16)
        first_other = jnp.concatenate([dot(m1, branch, 0, 0), dot(f1, d_c, 0, 0)], axis=1).astype(bf16)
        first_got = send(first_other, links.cores())
        first_own = jnp.concatenate([dot(m0, branch, 0, 0), dot(f0, d_c, 0, 0)], axis=1).astype(bf16)
        edge = after(edge, first_own)
        trail = jnp.concatenate([d_conv[1:], edge], axis=0)
        d_mixin = kernel[2] * d_conv + kernel[1] * trail[:rows] + kernel[0] * trail[1:]
        taps = [jnp.sum(d_conv * v, axis=0) for v in (back_two, back_one, mixed_in)]
        d_bx = jnp.concatenate([(d_mixin * v).astype(bf16) for v in (x_part, b_part)], axis=1)
        d_bx = after(d_bx, first_got, *[grouped[i] for i in grouped], *[shifted[i] for i in shifted])
        last_other = dot(f1, d_bx, 0, 0).astype(bf16)
        last_got = send(last_other, links.cores())
        last_own = dot(f0, d_bx, 0, 0).astype(bf16)
        grouped[T - 1] = group_sum(cored[T - 1][0], after(cored[T - 1][1], d_bx))
        if T > 1:
            shifted[T - 2] = shift_back(turn[T - 2], after(grouped[T - 2], d_bx))

        def pieces(v, parts):
            take = lambda i, k: v[:, i * C + k * chan : i * C + (k + 1) * chan]
            return [jnp.concatenate([take(i, k) for i in range(parts)], axis=1) for k in range(T)]

        def all_shifts(blocks):
            return blocks[0] + sum(shift_back(k, blocks[k]).astype(f32) for k in range(1, T))

        first_sum = all_shifts(pieces(walk_back(first_own, first_got), 2))
        last_sum = all_shifts(pieces(walk_back(last_own, last_got), 2))
        grad_out = first_sum[:, :chan]
        grad_in = jnp.stack([last_sum[:, :chan], first_sum[:, chan:], last_sum[:, chan:]], axis=1)

        d_proj = after(jnp.concatenate([d_bx[:, :C], d_c, d_bx[:, C:]], axis=1), last_got)
        d_first = jnp.concatenate([dot(d_proj, in0, 1, 1), dot(d_proj, in1, 1, 1)], axis=1)
        gain_one_part = jnp.sum(d_first * normed_one, axis=0)
        d_x = restore((d_resid + norm_back(d_first, normed_one, scale_one, gain_one)).astype(bf16))
        block_out = restore((resid + ffn[rows:] + ffn_theirs).astype(bf16))

        total = grouped[T - 1] + sum(shifted[i].astype(f32) for i in shifted)
        ours, yours = total[:, :block], send(total[:, block:].astype(bf16), links.flip(0)).astype(f32)
        low = jnp.where(me_x == 0, ours, yours)
        high = jnp.where(me_x == 0, yours, ours)
        grads = [
            jnp.concatenate([low[i * part : (i + 1) * part], high[i * part : (i + 1) * part]], axis=0) for i in range(3)
        ]

        taps = jnp.stack(taps)
        taps = lax.dynamic_slice_in_dim(jnp.concatenate([taps, taps], axis=1), C - me_t * chan, C, 1)
        small = jnp.concatenate([taps, restore_rows(gain_one_part)[None], restore_rows(gain_two_part)[None]], axis=0)
        small = small + send(small, links.cores())
        for j in range(links.bits):
            small = small + send(small, links.flip(j))
        k = 1
        while k < T:
            small = small + send(small, links.pairs(lambda d, t: (d, t ^ k)))
            k *= 2
        return (
            block_out,
            d_x,
            grad_in,
            grad_out.T,
            grads[0].T,
            grads[1].T,
            grads[2],
            small[:3],
            small[3],
            small[4],
        )

    return body


def solution(mesh):
    links = Links(mesh.shape["dp"], mesh.shape["tensor"])
    in_specs = (
        P(("dp", "tensor"), None),
        P("dp", None, "tensor"),
        P("tensor", "dp"),
        P("dp", "tensor"),
        P("dp", "tensor"),
        P("tensor", "dp"),
        P(),
        P(),
        P(),
        P(("dp", "tensor"), None),
    )
    out_specs = (
        P(("dp", "tensor"), None),
        P(("dp", "tensor"), None),
        P("dp", None, "tensor"),
        P("tensor", "dp"),
        P("dp", "tensor"),
        P("dp", "tensor"),
        P("tensor", "dp"),
        P(),
        P(),
        P(),
    )
    return jax.shard_map(
        make_body(links), mesh=mesh, in_specs=in_specs, out_specs=out_specs, check_vma=False
    )
```

```python
import jax
import jax.numpy as jnp
from jax import lax
from jax.experimental import pallas as pl
from jax.experimental.pallas import tpu as pltpu
from jax.sharding import PartitionSpec as P

LEN = 1024
epsilon = 1e-05
AXES = ("dp", "tensor")
bf16 = jnp.bfloat16
f32 = jnp.float32
INTERPRET = False


class Links:
    def __init__(self, dp, tensor):
        self.dp, self.tensor = dp, tensor
        self.bits = (dp // 2).bit_length() - 1
        assert dp == 2 << self.bits and self.bits >= 1
        self.devices = [(d, t) for d in range(dp) for t in range(tensor)]

    def at(self, d, t):
        return d * self.tensor + t

    def pairs(self, target):
        return [(self.at(d, t), self.at(*target(d, t))) for d, t in self.devices]

    def shift(self, k):
        return self.pairs(lambda d, t: (d, (t - k) % self.tensor))

    def bit(self, core, step):
        return step if core == 0 else self.bits - 1 - step

    def step(self, j):
        return self.pairs(lambda d, t: (d ^ (2 << self.bit(d % 2, j)), t))

    def flip(self, j):
        return self.pairs(lambda d, t: (d ^ (2 << j), t))

    def cores(self):
        return self.pairs(lambda d, t: (d ^ 1, t))

    def spread(self, p):
        return ((p << 1) | (p >> self.bits)) & (self.dp - 1)


def send(x, pairs):
    return lax.ppermute(x, AXES, pairs)


def dot(a, b, ca, cb):
    return lax.dot_general(a, b, (((ca,), (cb,)), ((), ())), preferred_element_type=f32)


def norm_rows(values):
    scale = lax.rsqrt(jnp.mean(values * values, axis=-1, keepdims=True) + epsilon)
    return (values * scale, scale)


def norm_back(grad_h, normed, scale, gain):
    grad_n = grad_h * gain
    inner = jnp.mean(grad_n * normed, axis=-1, keepdims=True)
    return scale * (grad_n - normed * inner)


def after(x, *others):
    return lax.optimization_barrier((x,) + others)[0]


def ffn_kernel(part, *refs):
    h_ref, g_ref, *w_refs = refs[:6]
    dh_ref, ffn_ref, own0_ref, own1_ref, other_ref, w_ref = refs[6:]
    both = 2 * part
    q = w_refs[0].shape[1]
    cut = [slice(i * q, (i + 1) * q) for i in range(4)]
    for w, c in zip(w_refs, cut):
        w_ref[:, c] = w[...]
    h, g = h_ref[...], g_ref[...]
    gate_up = dot(w_ref[:both], h, 1, 1)
    d_hidden = dot(w_ref[both:], g, 1, 1)
    gate, up = gate_up[:part], gate_up[part:]
    sigma = 1.0 / (1.0 + jnp.exp(-gate))
    silu = gate * sigma
    hidden = (silu * up).astype(bf16)
    d_gate = (d_hidden * up * sigma * (1.0 + gate * (1.0 - sigma))).astype(bf16)
    d_up = (d_hidden * silu).astype(bf16)
    d_both = jnp.concatenate([d_gate, d_up], axis=0)
    dh_ref[...] = dot(d_both, w_ref[:both], 0, 0).astype(bf16)
    ffn_ref[...] = dot(hidden, w_ref[both:], 0, 0).astype(bf16)
    for rows, a, b in ((slice(0, both), d_both, h), (slice(both, 3 * part), hidden, g)):
        grad = dot(a, b, 1, 0)
        own0_ref[rows] = grad[:, cut[0]].astype(bf16)
        own1_ref[rows] = grad[:, cut[1]].astype(bf16)
        other_ref[rows] = grad[:, 2 * q :].astype(bf16)


def ffn_chunk(h, g, weights):
    tokens, D = h.shape
    n, q = weights[0].shape
    part = n // 3

    def kernel(*refs):
        ffn_kernel(part, *refs)

    return pl.pallas_call(
        kernel,
        out_shape=[
            jax.ShapeDtypeStruct((tokens, D), bf16),
            jax.ShapeDtypeStruct((tokens, D), bf16),
            jax.ShapeDtypeStruct((n, q), bf16),
            jax.ShapeDtypeStruct((n, q), bf16),
            jax.ShapeDtypeStruct((n, 2 * q), bf16),
        ],
        scratch_shapes=[pltpu.VMEM((n, D), bf16)],
        compiler_params=pltpu.CompilerParams(vmem_limit_bytes=58 * 1024 * 1024),
        cost_estimate=pl.CostEstimate(
            flops=20 * tokens * D * part, bytes_accessed=12 * n * q * 2, transcendentals=tokens * part
        ),
        interpret=INTERPRET,
    )(h, g, *weights)


def make_body(links):
    dp, T = links.dp, links.tensor

    def body(x_in, in_w, out_w, gate_w, up_w, down_w, conv_w, gain1, gain2, d_out):
        rows, D = x_in.shape
        block = D // dp
        half = D // 2
        chan = in_w.shape[2]
        C = chan * T
        part = gate_w.shape[1] // 2
        per_seq = LEN // rows
        me_dp = lax.axis_index("dp")
        me_t = lax.axis_index("tensor")
        me_x = (me_dp // 2) % 2
        core = me_dp % 2
        groups = dp // 2
        canonical = [
            [sum(((q >> links.bit(c, j)) & 1) << j for j in range(links.bits)) for q in range(groups)] for c in (0, 1)
        ]
        walked = [[order.index(p) for p in range(groups)] for order in canonical]

        def by_core(blocks, order):
            a, b = order
            return [blocks[i] if i == j else jnp.where(core == 0, blocks[i], blocks[j]) for i, j in zip(a, b)]

        def walk_start(own, got):
            x = own.astype(f32) + got.astype(f32)
            return by_core([x[i * block : (i + 1) * block] for i in range(groups)], walked)

        def walk_send(blocks, j):
            return send(jnp.concatenate(blocks[len(blocks) // 2 :], axis=0).astype(bf16), links.step(j))

        def walk_add(blocks, got):
            return [
                blocks[i] + got[i * block : (i + 1) * block].astype(f32) for i in range(len(blocks) // 2)
            ]

        def shift_back(k, x):
            return send(x.astype(bf16), [(b, a) for a, b in links.shift(k)])

        def swap(v):
            parts = [v[:, (p ^ 1) * block : ((p ^ 1) + 1) * block] for p in range(dp)]
            return jnp.concatenate(parts, axis=1)

        mine = me_dp ^ jnp.asarray([links.spread(p) for p in range(dp)], jnp.int32)
        source = (mine[:, None] * block + jnp.arange(block)[None, :]).reshape(D)
        place = (jnp.arange(D)[:, None] == source[None, :]).astype(bf16)

        def arrange(v):
            return dot(v, place, 1, 0).astype(bf16)

        def restore(v):
            return dot(v, place, 1, 1).astype(bf16)

        def restore_rows(v):
            return jnp.sum(
                jnp.where((mine[None, :] == jnp.arange(dp)[:, None])[:, :, None], v.reshape(1, dp, block), 0.0), axis=1
            ).reshape(D)

        in_own = in_w.reshape(block, 3 * chan)
        in_k = [in_own] + [send(in_own, links.shift(k)) for k in range(1, T)]
        stack = jnp.concatenate([w.reshape(2, part, block) for w in (gate_w.T, up_w.T, down_w)], axis=1)
        ffn_keep = jnp.where(me_x == 0, stack[0], stack[1])
        ffn_give = jnp.where(me_x == 0, stack[1], stack[0])
        ffn_own = jnp.concatenate([ffn_keep, send(ffn_give, links.flip(0))], axis=1)

        own = [ffn_own]
        near = [[] for _ in range(T)]

        def shift_chunk(*waits):
            if len(own) < T:
                own.append(send(after(own[-1], *waits), links.shift(1)))

        def exchange(k, *waits):
            if k < T:
                x = after(own[k], *waits)
                for j in range(1, links.bits):
                    got = send(x, links.flip(j))
                    near[k] = [x, got]
                    if j < links.bits - 1:
                        x = jnp.concatenate(near[k], axis=1)

        def walk_first(x):
            return [x, send(x, links.step(0))]

        def walk_rest(blocks, *waits):
            for j in range(1, links.bits):
                whole = jnp.concatenate(blocks, axis=0)
                if j == 1:
                    whole = after(whole, *waits)
                blocks = blocks + [send(whole, links.step(j))]
            return blocks

        def in_order(wholes):
            blocks = [w[i * block : (i + 1) * block] for w in wholes for i in range(w.shape[0] // block)]
            return jnp.concatenate(by_core(blocks, canonical), axis=0)

        in_cols = jnp.concatenate([w[:, i * chan : (i + 1) * chan] for i in range(3) for w in in_k], axis=1)
        in_cols = after(in_cols, ffn_own)
        in_first = walk_first(in_cols)
        out_own = after(out_w.T, in_cols)
        out_k = [out_own] + [send(out_own, links.shift(k)) for k in range(1, T)]
        out_cols = jnp.concatenate(out_k, axis=1)
        slot2 = [in_first[1], out_cols]
        in_walked = walk_rest(in_first, *slot2)
        out_first = walk_first(after(out_cols, *slot2))
        shift_chunk(*slot2)
        slot3 = [in_walked[-1], own[-1], out_first[1]]
        in0 = after(in_order(in_walked), *slot3)
        in1 = send(in0, links.cores())
        out_walked = walk_rest(out_first, *slot3)
        shift_chunk(*slot3)
        exchange(1, *slot3, out_walked[-1])
        out0 = in_order(out_walked)
        out1 = send(out0, links.cores())

        tokens = arrange(x_in).astype(f32)
        cot16 = arrange(d_out)
        partner_cot = send(after(swap(cot16), *slot3, out_walked[-1]), links.flip(0))
        gains = arrange(jnp.stack([gain1, gain2])).astype(f32)
        gain_one, gain_two = gains[0], gains[1]
        turned = jnp.concatenate([conv_w, conv_w], axis=1)
        kernel = lax.dynamic_slice_in_dim(turned, me_t * chan, C, 1).astype(f32)

        def split(a, axis=1):
            return lax.slice_in_dim(a, 0, half, axis=axis), lax.slice_in_dim(a, half, D, axis=axis)

        normed_one, scale_one = norm_rows(tokens)
        first = (normed_one * gain_one).astype(bf16)
        f0, f1 = split(first)
        projected = dot(f0, in0, 1, 0) + dot(f1, in1, 1, 0)
        b_part, c_part, x_part = projected[:, :C], projected[:, C : 2 * C], projected[:, 2 * C :]
        mixed_in = b_part * x_part
        follows = [(links.at(d, t), links.at(d, t + 1)) for d, t in links.devices if (t + 1) % per_seq]
        no_rows = jnp.zeros((2, C), f32)
        before = send(jnp.roll(mixed_in[rows - 2 :], -chan, axis=1), follows) if follows else no_rows
        lead = jnp.concatenate([before, mixed_in[: rows - 1]], axis=0)
        back_one = lead[1:]
        back_two = lead[:rows]
        conv_out = kernel[2] * mixed_in + kernel[1] * back_one + kernel[0] * back_two
        branch = (c_part * conv_out).astype(bf16)
        slot4 = [out_walked[-1], own[-1], partner_cot] + near[1 % T]
        branch = after(branch, *slot4)
        exchange(2, branch)
        shift_chunk(branch)
        resid = tokens + jnp.concatenate([dot(branch, out0, 1, 1), dot(branch, out1, 1, 1)], axis=1)
        normed_two, scale_two = norm_rows(resid)
        second = (normed_two * gain_two).astype(bf16)
        cot_all = jnp.concatenate([partner_cot, cot16], axis=0)
        second_all = jnp.concatenate([send(swap(second), links.flip(0)), second], axis=0)

        def core_sum(own0, own1, other):
            got = send(other, links.cores())
            return [own0, got[:, : half // 2]], (own1.astype(f32) + got[:, half // 2 :].astype(f32)).astype(bf16)

        def group_sum(kept, sent):
            got = send(sent, links.flip(links.bits - 1))
            if links.bits == 2:
                return (lambda: sum(v.astype(f32) for v in kept + [got])), got
            x = sum(v.astype(f32) for v in kept + [got])
            for j in reversed(range(1, links.bits - 1)):
                n = x.shape[1] // 2
                got = send(x[:, n:].astype(bf16), links.flip(j))
                x = x[:, :n] + got.astype(f32)
            return (lambda: x), got

        def shift_sum(i, *waits):
            return shift_back(turn[i], after(grouped[i][0]().astype(bf16), *waits))

        def other_core(k):
            return near[k] + [send(x, links.cores()) for x in near[k]]

        turn = list(range(1, T)) + [0]
        d_h, ffn, sums, cored, grouped, shifted, weights = {}, {}, {}, {}, {}, {}, {}
        weights[turn[0]] = other_core(turn[0])
        slot = weights[turn[0]] + [x for k in turn[:2] for x in near[k]] + own
        for i, k in enumerate(turn):
            h_in = after(second_all, *slot)
            slot = []
            if i + 2 < T:
                exchange(turn[i + 2], h_in)
                slot += near[turn[i + 2]]
            if i + 1 < T:
                weights[turn[i + 1]] = other_core(turn[i + 1])
                slot += weights[turn[i + 1]]
            if i >= 1:
                cored[i - 1] = core_sum(*sums[i - 1])
                slot.append(cored[i - 1][1])
            if i >= 2:
                grouped[i - 2] = group_sum(cored[i - 2][0], after(cored[i - 2][1], h_in))
                slot.append(grouped[i - 2][1])
            if i >= 3:
                shifted[i - 3] = shift_sum(i - 3, h_in)
                slot.append(shifted[i - 3])
            d_h[k], ffn[k], *sums[i] = ffn_chunk(h_in, cot_all, weights[k])
            sums[i][2] = after(sums[i][2], *slot)

        def total(parts, rows_of):
            return sum(parts[k][rows_of].astype(f32) for k in turn)

        theirs, ours = slice(0, rows), slice(rows, 2 * rows)
        got = send(swap(total(d_h, theirs).astype(bf16)), links.flip(0))
        cored[T - 1] = core_sum(*sums[T - 1])
        if T > 1:
            grouped[T - 2] = group_sum(cored[T - 2][0], after(cored[T - 2][1], cored[T - 1][1]))
        if T > 2:
            shifted[T - 3] = shift_sum(T - 3, sums[T - 1][2])
        ffn_theirs = swap(total(ffn, theirs).astype(bf16))
        got = after(got, ffn_theirs, cored[T - 1][1], *[grouped[i][1] for i in grouped])
        d_second = total(d_h, ours) + got.astype(f32)
        ffn_sent = send(after(ffn_theirs, got), links.flip(0))
        grouped[T - 1] = group_sum(cored[T - 1][0], after(cored[T - 1][1], got))

        gain_two_part = jnp.sum(d_second * normed_two, axis=0)
        d_resid = cot16.astype(f32) + norm_back(d_second, normed_two, scale_two, gain_two)
        d_mixed = d_resid.astype(bf16)
        m0, m1 = split(d_mixed)
        d_branch = dot(m0, out0, 1, 0) + dot(m1, out1, 1, 0)
        d_conv = d_branch * c_part
        d_c = d_branch * conv_out
        leads = [(b, a) for a, b in follows]
        edge = send(jnp.roll(d_conv[:2], chan, axis=1), leads) if leads else no_rows
        d_c = d_c.astype(bf16)
        first_other = jnp.concatenate([dot(m1, branch, 0, 0), dot(f1, d_c, 0, 0)], axis=1).astype(bf16)
        first_got = send(first_other, links.cores())
        m0 = after(m0, grouped[T - 1][1])
        first_own = jnp.concatenate([dot(m0, branch, 0, 0), dot(f0, d_c, 0, 0)], axis=1).astype(bf16)
        edge = after(edge, first_own)
        if T > 1:
            shifted[T - 2] = shift_sum(T - 2, edge)
        first_blocks = walk_start(first_own, first_got)
        trail = jnp.concatenate([d_conv[1:], edge], axis=0)
        d_mixin = kernel[2] * d_conv + kernel[1] * trail[:rows] + kernel[0] * trail[1:]
        taps = [jnp.sum(d_conv * v, axis=0) for v in (back_two, back_one, mixed_in)]
        d_bx = jnp.concatenate([(d_mixin * v).astype(bf16) for v in (x_part, b_part)], axis=1)
        d_bx = after(d_bx, *first_blocks, *[shifted[i] for i in range(T - 2)])
        last_other = dot(f1, d_bx, 0, 0).astype(bf16)
        last_got = send(last_other, links.cores())
        last_own = dot(after(f0, last_other, ffn_sent), d_bx, 0, 0).astype(bf16)
        d_proj = jnp.concatenate([d_bx[:, :C], d_c, d_bx[:, C:]], axis=1)
        d_proj = after(d_proj, last_own)
        d_first = jnp.concatenate([dot(d_proj, in0, 1, 1), dot(d_proj, in1, 1, 1)], axis=1)
        *first_blocks, last_got, d_first = lax.optimization_barrier((*first_blocks, last_got, d_first))
        first_got = walk_send(first_blocks, links.bits - 1)
        last_blocks = walk_start(last_own, last_got)
        for j in reversed(range(links.bits)):
            last_got = walk_send(last_blocks, j)
            if j == links.bits - 1:
                tail = last_got
            first_blocks = walk_add(first_blocks, first_got)
            if j:
                first_got = walk_send(first_blocks, j - 1)
            last_blocks = walk_add(last_blocks, last_got)

        def pieces(v, parts):
            take = lambda i, k: v[:, i * C + k * chan : i * C + (k + 1) * chan]
            return [jnp.concatenate([take(i, k) for i in range(parts)], axis=1) for k in range(T)]

        def all_shifts(blocks):
            return blocks[0] + sum(shift_back(k, blocks[k]).astype(f32) for k in range(1, T))

        first_sum = all_shifts(pieces(first_blocks[0], 2))
        last_sum = all_shifts(pieces(last_blocks[0], 2))
        grad_out = first_sum[:, :chan]
        grad_in = jnp.stack([last_sum[:, :chan], first_sum[:, chan:], last_sum[:, chan:]], axis=1)

        gain_one_part = jnp.sum(d_first * normed_one, axis=0)
        d_x = restore((d_resid + norm_back(d_first, normed_one, scale_one, gain_one)).astype(bf16))
        block_out = restore((resid + total(ffn, ours) + after(ffn_sent, last_got).astype(f32)).astype(bf16))

        pieces_back = [after(shifted[i], tail) for i in shifted]
        ffn_sum = after(grouped[T - 1][0](), tail) + sum(v.astype(f32) for v in pieces_back)
        mine_sum = ffn_sum[:, :block]
        partner_sum = send(after(ffn_sum[:, block:].astype(bf16), last_got), links.flip(0)).astype(f32)
        low = jnp.where(me_x == 0, mine_sum, partner_sum)
        high = jnp.where(me_x == 0, partner_sum, mine_sum)
        grads = [
            jnp.concatenate([low[i * part : (i + 1) * part], high[i * part : (i + 1) * part]], axis=0) for i in range(3)
        ]

        taps = jnp.stack(taps)
        taps = lax.dynamic_slice_in_dim(jnp.concatenate([taps, taps], axis=1), C - me_t * chan, C, 1)
        small = jnp.concatenate([taps, restore_rows(gain_one_part)[None], restore_rows(gain_two_part)[None]], axis=0)
        small = small + send(small, links.cores())
        small = after(small, tail)
        for j in range(links.bits):
            small = small + send(small, links.flip(j))
        k = 1
        while k < T:
            small = small + send(small, links.pairs(lambda d, t: (d, t ^ k)))
            k *= 2
        return (
            block_out,
            d_x,
            grad_in,
            grad_out.T,
            grads[0].T,
            grads[1].T,
            grads[2],
            small[:3],
            small[3],
            small[4],
        )

    return body


def solution(mesh):
    links = Links(mesh.shape["dp"], mesh.shape["tensor"])
    in_specs = (
        P(("dp", "tensor"), None),
        P("dp", None, "tensor"),
        P("tensor", "dp"),
        P("dp", "tensor"),
        P("dp", "tensor"),
        P("tensor", "dp"),
        P(),
        P(),
        P(),
        P(("dp", "tensor"), None),
    )
    out_specs = (
        P(("dp", "tensor"), None),
        P(("dp", "tensor"), None),
        P("dp", None, "tensor"),
        P("tensor", "dp"),
        P("dp", "tensor"),
        P("dp", "tensor"),
        P("tensor", "dp"),
        P(),
        P(),
        P(),
    )
    return jax.shard_map(
        make_body(links), mesh=mesh, in_specs=in_specs, out_specs=out_specs, check_vma=False
    )
```

```python
import jax
import jax.numpy as jnp
from jax import lax
from jax.experimental import pallas as pl
from jax.experimental.pallas import tpu as pltpu
from jax.sharding import PartitionSpec as P

LEN = 1024
epsilon = 1e-05
AXES = ("dp", "tensor")
bf16 = jnp.bfloat16
f32 = jnp.float32
INTERPRET = False


class Links:
    def __init__(self, dp, tensor):
        self.dp, self.tensor = dp, tensor
        self.bits = (dp // 2).bit_length() - 1
        assert dp == 2 << self.bits and self.bits >= 1
        self.devices = [(d, t) for d in range(dp) for t in range(tensor)]

    def at(self, d, t):
        return d * self.tensor + t

    def pairs(self, target):
        return [(self.at(d, t), self.at(*target(d, t))) for d, t in self.devices]

    def shift(self, k):
        return self.pairs(lambda d, t: (d, (t - k) % self.tensor))

    def bit(self, core, step):
        return step if core == 0 else self.bits - 1 - step

    def step(self, j):
        return self.pairs(lambda d, t: (d ^ (2 << self.bit(d % 2, j)), t))

    def flip(self, j):
        return self.pairs(lambda d, t: (d ^ (2 << j), t))

    def cores(self):
        return self.pairs(lambda d, t: (d ^ 1, t))

    def spread(self, p):
        return ((p << 1) | (p >> self.bits)) & (self.dp - 1)


def send(x, pairs):
    return lax.ppermute(x, AXES, pairs)


def dot(a, b, ca, cb):
    return lax.dot_general(a, b, (((ca,), (cb,)), ((), ())), preferred_element_type=f32)


def norm_rows(values):
    scale = lax.rsqrt(jnp.mean(values * values, axis=-1, keepdims=True) + epsilon)
    return (values * scale, scale)


def norm_back(grad_h, normed, scale, gain):
    grad_n = grad_h * gain
    inner = jnp.mean(grad_n * normed, axis=-1, keepdims=True)
    return scale * (grad_n - normed * inner)


def after(x, *others):
    return lax.optimization_barrier((x,) + others)[0]


def ffn_kernel(part, *refs):
    h_ref, g_ref, *w_refs = refs[:6]
    dh_ref, ffn_ref, own0_ref, own1_ref, other_ref, w_ref = refs[6:]
    both = 2 * part
    q = w_refs[0].shape[1]
    cut = [slice(i * q, (i + 1) * q) for i in range(4)]
    for w, c in zip(w_refs, cut):
        w_ref[:, c] = w[...]
    h, g = h_ref[...], g_ref[...]
    gate_up = dot(w_ref[:both], h, 1, 1)
    d_hidden = dot(w_ref[both:], g, 1, 1)
    gate, up = gate_up[:part], gate_up[part:]
    sigma = 1.0 / (1.0 + jnp.exp(-gate))
    silu = gate * sigma
    hidden = (silu * up).astype(bf16)
    d_gate = (d_hidden * up * sigma * (1.0 + gate * (1.0 - sigma))).astype(bf16)
    d_up = (d_hidden * silu).astype(bf16)
    d_both = jnp.concatenate([d_gate, d_up], axis=0)
    dh_ref[...] = dot(d_both, w_ref[:both], 0, 0).astype(bf16)
    ffn_ref[...] = dot(hidden, w_ref[both:], 0, 0).astype(bf16)
    for rows, a, b in ((slice(0, both), d_both, h), (slice(both, 3 * part), hidden, g)):
        grad = dot(a, b, 1, 0)
        own0_ref[rows] = grad[:, cut[0]].astype(bf16)
        own1_ref[rows] = grad[:, cut[1]].astype(bf16)
        other_ref[rows] = grad[:, 2 * q :].astype(bf16)


def ffn_chunk(h, g, weights):
    tokens, D = h.shape
    n, q = weights[0].shape
    part = n // 3

    def kernel(*refs):
        ffn_kernel(part, *refs)

    return pl.pallas_call(
        kernel,
        out_shape=[
            jax.ShapeDtypeStruct((tokens, D), bf16),
            jax.ShapeDtypeStruct((tokens, D), bf16),
            jax.ShapeDtypeStruct((n, q), bf16),
            jax.ShapeDtypeStruct((n, q), bf16),
            jax.ShapeDtypeStruct((n, 2 * q), bf16),
        ],
        scratch_shapes=[pltpu.VMEM((n, D), bf16)],
        compiler_params=pltpu.CompilerParams(vmem_limit_bytes=58 * 1024 * 1024),
        cost_estimate=pl.CostEstimate(
            flops=20 * tokens * D * part, bytes_accessed=12 * n * q * 2, transcendentals=tokens * part
        ),
        interpret=INTERPRET,
    )(h, g, *weights)


def make_body(links):
    dp, T = links.dp, links.tensor

    def body(x_in, in_w, out_w, gate_w, up_w, down_w, conv_w, gain1, gain2, d_out):
        rows, D = x_in.shape
        block = D // dp
        half = D // 2
        chan = in_w.shape[2]
        C = chan * T
        part = gate_w.shape[1] // 2
        per_seq = LEN // rows
        me_dp = lax.axis_index("dp")
        me_t = lax.axis_index("tensor")
        me_x = (me_dp // 2) % 2
        core = me_dp % 2
        groups = dp // 2
        canonical = [
            [sum(((q >> links.bit(c, j)) & 1) << j for j in range(links.bits)) for q in range(groups)] for c in (0, 1)
        ]
        walked = [[order.index(p) for p in range(groups)] for order in canonical]

        def by_core(blocks, order):
            a, b = order
            return [blocks[i] if i == j else jnp.where(core == 0, blocks[i], blocks[j]) for i, j in zip(a, b)]

        def walk_start(own, got):
            x = own.astype(f32) + got.astype(f32)
            return by_core([x[i * block : (i + 1) * block] for i in range(groups)], walked)

        def walk_send(blocks, j):
            return send(jnp.concatenate(blocks[len(blocks) // 2 :], axis=0).astype(bf16), links.step(j))

        def walk_add(blocks, got):
            return [
                blocks[i] + got[i * block : (i + 1) * block].astype(f32) for i in range(len(blocks) // 2)
            ]

        def shift_back(k, x):
            return send(x.astype(bf16), [(b, a) for a, b in links.shift(k)])

        def swap(v):
            parts = [v[:, (p ^ 1) * block : ((p ^ 1) + 1) * block] for p in range(dp)]
            return jnp.concatenate(parts, axis=1)

        mine = me_dp ^ jnp.asarray([links.spread(p) for p in range(dp)], jnp.int32)
        source = (mine[:, None] * block + jnp.arange(block)[None, :]).reshape(D)
        place = (jnp.arange(D)[:, None] == source[None, :]).astype(bf16)

        def arrange(v):
            return dot(v, place, 1, 0).astype(bf16)

        def restore(v):
            return dot(v, place, 1, 1).astype(bf16)

        def restore_rows(v):
            return jnp.sum(
                jnp.where((mine[None, :] == jnp.arange(dp)[:, None])[:, :, None], v.reshape(1, dp, block), 0.0), axis=1
            ).reshape(D)

        in_own = in_w.reshape(block, 3 * chan)
        in_k = [in_own] + [send(in_own, links.shift(k)) for k in range(1, T)]
        stack = jnp.concatenate([w.reshape(2, part, block) for w in (gate_w.T, up_w.T, down_w)], axis=1)
        ffn_keep = jnp.where(me_x == 0, stack[0], stack[1])
        ffn_give = jnp.where(me_x == 0, stack[1], stack[0])
        ffn_own = jnp.concatenate([ffn_keep, send(ffn_give, links.flip(0))], axis=1)

        own = [ffn_own]
        near = [[] for _ in range(T)]

        def shift_chunk(*waits):
            if len(own) < T:
                own.append(send(after(own[-1], *waits), links.shift(1)))

        def exchange(k, *waits):
            if k < T:
                x = after(own[k], *waits)
                for j in range(1, links.bits):
                    got = send(x, links.flip(j))
                    near[k] = [x, got]
                    if j < links.bits - 1:
                        x = jnp.concatenate(near[k], axis=1)

        def walk_first(x):
            return [x, send(x, links.step(0))]

        def walk_rest(blocks, *waits):
            for j in range(1, links.bits):
                whole = jnp.concatenate(blocks, axis=0)
                if j == 1:
                    whole = after(whole, *waits)
                blocks = blocks + [send(whole, links.step(j))]
            return blocks

        def in_order(wholes):
            blocks = [w[i * block : (i + 1) * block] for w in wholes for i in range(w.shape[0] // block)]
            return jnp.concatenate(by_core(blocks, canonical), axis=0)

        in_cols = jnp.concatenate([w[:, i * chan : (i + 1) * chan] for i in range(3) for w in in_k], axis=1)
        x_arranged, cot16 = arrange(x_in), arrange(d_out)
        in_cols = after(in_cols, ffn_own, x_arranged, cot16)
        in_first = walk_first(in_cols)
        out_own = after(out_w.T, in_cols)
        out_k = [out_own] + [send(out_own, links.shift(k)) for k in range(1, T)]
        out_cols = jnp.concatenate(out_k, axis=1)
        slot2 = [in_first[1], out_cols]
        in_walked = walk_rest(in_first, *slot2)
        out_first = walk_first(after(out_cols, *slot2))
        shift_chunk(*slot2)
        slot3 = [in_walked[-1], own[-1], out_first[1]]
        in0 = after(in_order(in_walked), *slot3)
        in1 = send(in0, links.cores())
        out_walked = walk_rest(out_first, *slot3)
        shift_chunk(*slot3)
        exchange(1, *slot3, out_walked[-1])
        out0 = in_order(out_walked)
        out1 = send(out0, links.cores())

        tokens = x_arranged.astype(f32)
        partner_cot = send(after(swap(cot16), *slot3, out_walked[-1]), links.flip(0))
        gains = arrange(jnp.stack([gain1, gain2])).astype(f32)
        gain_one, gain_two = gains[0], gains[1]
        turned = jnp.concatenate([conv_w, conv_w], axis=1)
        kernel = lax.dynamic_slice_in_dim(turned, me_t * chan, C, 1).astype(f32)

        def split(a, axis=1):
            return lax.slice_in_dim(a, 0, half, axis=axis), lax.slice_in_dim(a, half, D, axis=axis)

        normed_one, scale_one = norm_rows(tokens)
        first = (normed_one * gain_one).astype(bf16)
        f0, f1 = split(first)
        projected = dot(f0, in0, 1, 0) + dot(f1, in1, 1, 0)
        b_part, c_part, x_part = projected[:, :C], projected[:, C : 2 * C], projected[:, 2 * C :]
        mixed_in = b_part * x_part
        follows = [(links.at(d, t), links.at(d, t + 1)) for d, t in links.devices if (t + 1) % per_seq]
        no_rows = jnp.zeros((2, C), f32)
        before = send(jnp.roll(mixed_in[rows - 2 :], -chan, axis=1), follows) if follows else no_rows
        lead = jnp.concatenate([before, mixed_in[: rows - 1]], axis=0)
        back_one = lead[1:]
        back_two = lead[:rows]
        conv_out = kernel[2] * mixed_in + kernel[1] * back_one + kernel[0] * back_two
        branch = (c_part * conv_out).astype(bf16)
        slot4 = [out_walked[-1], own[-1], partner_cot] + near[1 % T]
        branch = after(branch, *slot4)
        exchange(2, branch)
        shift_chunk(branch)
        resid = tokens + jnp.concatenate([dot(branch, out0, 1, 1), dot(branch, out1, 1, 1)], axis=1)
        normed_two, scale_two = norm_rows(resid)
        second = (normed_two * gain_two).astype(bf16)
        cot_all = jnp.concatenate([partner_cot, cot16], axis=0)
        second_all = jnp.concatenate([send(swap(second), links.flip(0)), second], axis=0)

        def core_sum(own0, own1, other):
            got = send(other, links.cores())
            return [own0, got[:, : half // 2]], (own1.astype(f32) + got[:, half // 2 :].astype(f32)).astype(bf16)

        def group_sum(kept, sent):
            got = send(sent, links.flip(links.bits - 1))
            if links.bits == 2:
                return (lambda: sum(v.astype(f32) for v in kept + [got])), got
            x = sum(v.astype(f32) for v in kept + [got])
            for j in reversed(range(1, links.bits - 1)):
                n = x.shape[1] // 2
                got = send(x[:, n:].astype(bf16), links.flip(j))
                x = x[:, :n] + got.astype(f32)
            return (lambda: x), got

        def shift_sum(i, *waits):
            return shift_back(turn[i], after(grouped[i][0]().astype(bf16), *waits))

        def other_core(k):
            return near[k] + [send(x, links.cores()) for x in near[k]]

        turn = list(range(1, T)) + [0]
        d_h, ffn, sums, cored, grouped, shifted, weights = {}, {}, {}, {}, {}, {}, {}
        weights[turn[0]] = other_core(turn[0])
        slot = weights[turn[0]] + [x for k in turn[:2] for x in near[k]] + own
        for i, k in enumerate(turn):
            h_in = after(second_all, *slot)
            slot = []
            if i + 2 < T:
                exchange(turn[i + 2], h_in)
                slot += near[turn[i + 2]]
            if i + 1 < T:
                weights[turn[i + 1]] = other_core(turn[i + 1])
                slot += weights[turn[i + 1]]
            if i >= 1:
                cored[i - 1] = core_sum(*sums[i - 1])
                slot.append(cored[i - 1][1])
            if i >= 2:
                grouped[i - 2] = group_sum(cored[i - 2][0], after(cored[i - 2][1], h_in))
                slot.append(grouped[i - 2][1])
            if i >= 3:
                shifted[i - 3] = shift_sum(i - 3, h_in)
                slot.append(shifted[i - 3])
            d_h[k], ffn[k], *sums[i] = ffn_chunk(h_in, cot_all, weights[k])
            sums[i][2] = after(sums[i][2], *slot)

        def total(parts, rows_of):
            return sum(parts[k][rows_of].astype(f32) for k in turn)

        theirs, ours = slice(0, rows), slice(rows, 2 * rows)
        got = send(swap(total(d_h, theirs).astype(bf16)), links.flip(0))
        cored[T - 1] = core_sum(*sums[T - 1])
        if T > 1:
            grouped[T - 2] = group_sum(cored[T - 2][0], after(cored[T - 2][1], cored[T - 1][1]))
        if T > 2:
            shifted[T - 3] = shift_sum(T - 3, sums[T - 1][2])
        ffn_theirs = swap(total(ffn, theirs).astype(bf16))
        got = after(got, ffn_theirs, cored[T - 1][1], *[grouped[i][1] for i in grouped])
        d_second = total(d_h, ours) + got.astype(f32)
        ffn_sent = send(after(ffn_theirs, got), links.flip(0))
        grouped[T - 1] = group_sum(cored[T - 1][0], after(cored[T - 1][1], got))

        gain_two_part = jnp.sum(d_second * normed_two, axis=0)
        d_resid = cot16.astype(f32) + norm_back(d_second, normed_two, scale_two, gain_two)
        d_mixed = d_resid.astype(bf16)
        m0, m1 = split(d_mixed)
        d_branch = dot(m0, out0, 1, 0) + dot(m1, out1, 1, 0)
        d_conv = d_branch * c_part
        d_c = d_branch * conv_out
        leads = [(b, a) for a, b in follows]
        edge = send(jnp.roll(d_conv[:2], chan, axis=1), leads) if leads else no_rows
        d_c = d_c.astype(bf16)
        first_other = jnp.concatenate([dot(m1, branch, 0, 0), dot(f1, d_c, 0, 0)], axis=1).astype(bf16)
        first_got = send(first_other, links.cores())
        m0 = after(m0, grouped[T - 1][1])
        first_own = jnp.concatenate([dot(m0, branch, 0, 0), dot(f0, d_c, 0, 0)], axis=1).astype(bf16)
        edge = after(edge, first_own)
        if T > 1:
            shifted[T - 2] = shift_sum(T - 2, edge)
        first_blocks = walk_start(first_own, first_got)
        trail = jnp.concatenate([d_conv[1:], edge], axis=0)
        d_mixin = kernel[2] * d_conv + kernel[1] * trail[:rows] + kernel[0] * trail[1:]
        taps = [jnp.sum(d_conv * v, axis=0) for v in (back_two, back_one, mixed_in)]
        d_bx = jnp.concatenate([(d_mixin * v).astype(bf16) for v in (x_part, b_part)], axis=1)
        d_bx = after(d_bx, *first_blocks, *[shifted[i] for i in range(T - 2)])
        last_other = dot(f1, d_bx, 0, 0).astype(bf16)
        last_got = send(last_other, links.cores())
        last_own = dot(after(f0, last_other, ffn_sent), d_bx, 0, 0).astype(bf16)
        d_proj = jnp.concatenate([d_bx[:, :C], d_c, d_bx[:, C:]], axis=1)
        d_proj = after(d_proj, last_own)
        d_first = jnp.concatenate([dot(d_proj, in0, 1, 1), dot(d_proj, in1, 1, 1)], axis=1)
        *first_blocks, last_got, d_first = lax.optimization_barrier((*first_blocks, last_got, d_first))
        first_got = walk_send(first_blocks, links.bits - 1)
        last_blocks = walk_start(last_own, last_got)
        for j in reversed(range(links.bits)):
            last_got = walk_send(last_blocks, j)
            if j == links.bits - 1:
                tail = last_got
            first_blocks = walk_add(first_blocks, first_got)
            if j:
                first_got = walk_send(first_blocks, j - 1)
            last_blocks = walk_add(last_blocks, last_got)

        def pieces(v, parts):
            take = lambda i, k: v[:, i * C + k * chan : i * C + (k + 1) * chan]
            return [jnp.concatenate([take(i, k) for i in range(parts)], axis=1) for k in range(T)]

        def all_shifts(blocks):
            return blocks[0] + sum(shift_back(k, blocks[k]).astype(f32) for k in range(1, T))

        first_sum = all_shifts(pieces(first_blocks[0], 2))
        last_sum = all_shifts(pieces(last_blocks[0], 2))
        grad_out = first_sum[:, :chan]
        grad_in = jnp.stack([last_sum[:, :chan], first_sum[:, chan:], last_sum[:, chan:]], axis=1)

        gain_one_part = jnp.sum(d_first * normed_one, axis=0)
        d_x = restore((d_resid + norm_back(d_first, normed_one, scale_one, gain_one)).astype(bf16))
        block_out = restore((resid + total(ffn, ours) + after(ffn_sent, last_got).astype(f32)).astype(bf16))

        pieces_back = [after(shifted[i], tail) for i in shifted]
        ffn_sum = after(grouped[T - 1][0](), tail) + sum(v.astype(f32) for v in pieces_back)
        mine_sum = ffn_sum[:, :block]
        partner_sum = send(after(ffn_sum[:, block:].astype(bf16), last_got), links.flip(0)).astype(f32)
        low = jnp.where(me_x == 0, mine_sum, partner_sum)
        high = jnp.where(me_x == 0, partner_sum, mine_sum)
        grads = [
            jnp.concatenate([low[i * part : (i + 1) * part], high[i * part : (i + 1) * part]], axis=0) for i in range(3)
        ]

        taps = jnp.stack(taps)
        taps = lax.dynamic_slice_in_dim(jnp.concatenate([taps, taps], axis=1), C - me_t * chan, C, 1)
        small = jnp.concatenate([taps, restore_rows(gain_one_part)[None], restore_rows(gain_two_part)[None]], axis=0)
        small = small + send(small, links.cores())
        small = after(small, tail)
        for j in range(links.bits):
            small = small + send(small, links.flip(j))
        k = 1
        while k < T:
            small = small + send(small, links.pairs(lambda d, t: (d, t ^ k)))
            k *= 2
        return (
            block_out,
            d_x,
            grad_in,
            grad_out.T,
            grads[0].T,
            grads[1].T,
            grads[2],
            small[:3],
            small[3],
            small[4],
        )

    return body


def solution(mesh):
    links = Links(mesh.shape["dp"], mesh.shape["tensor"])
    in_specs = (
        P(("dp", "tensor"), None),
        P("dp", None, "tensor"),
        P("tensor", "dp"),
        P("dp", "tensor"),
        P("dp", "tensor"),
        P("tensor", "dp"),
        P(),
        P(),
        P(),
        P(("dp", "tensor"), None),
    )
    out_specs = (
        P(("dp", "tensor"), None),
        P(("dp", "tensor"), None),
        P("dp", None, "tensor"),
        P("tensor", "dp"),
        P("dp", "tensor"),
        P("dp", "tensor"),
        P("tensor", "dp"),
        P(),
        P(),
        P(),
    )
    return jax.shard_map(
        make_body(links), mesh=mesh, in_specs=in_specs, out_specs=out_specs, check_vma=False
    )
```

```python
import jax
import jax.numpy as jnp
from jax import lax
from jax.experimental import pallas as pl
from jax.experimental.pallas import tpu as pltpu
from jax.sharding import PartitionSpec as P

LEN = 1024
epsilon = 1e-05
AXES = ("dp", "tensor")
bf16 = jnp.bfloat16
f32 = jnp.float32
INTERPRET = False


class Links:
    def __init__(self, dp, tensor):
        self.dp, self.tensor = dp, tensor
        self.bits = (dp // 2).bit_length() - 1
        assert dp == 2 << self.bits and self.bits >= 1
        self.devices = [(d, t) for d in range(dp) for t in range(tensor)]

    def at(self, d, t):
        return d * self.tensor + t

    def pairs(self, target):
        return [(self.at(d, t), self.at(*target(d, t))) for d, t in self.devices]

    def shift(self, k):
        return self.pairs(lambda d, t: (d, (t - k) % self.tensor))

    def bit(self, core, step):
        return step if core == 0 else self.bits - 1 - step

    def step(self, j):
        return self.pairs(lambda d, t: (d ^ (2 << self.bit(d % 2, j)), t))

    def flip(self, j):
        return self.pairs(lambda d, t: (d ^ (2 << j), t))

    def cores(self):
        return self.pairs(lambda d, t: (d ^ 1, t))

    def spread(self, p):
        return ((p << 1) | (p >> self.bits)) & (self.dp - 1)


def send(x, pairs):
    return lax.ppermute(x, AXES, pairs)


def dot(a, b, ca, cb):
    return lax.dot_general(a, b, (((ca,), (cb,)), ((), ())), preferred_element_type=f32)


def norm_rows(values):
    scale = lax.rsqrt(jnp.mean(values * values, axis=-1, keepdims=True) + epsilon)
    return (values * scale, scale)


def norm_back(grad_h, normed, scale, gain):
    grad_n = grad_h * gain
    inner = jnp.mean(grad_n * normed, axis=-1, keepdims=True)
    return scale * (grad_n - normed * inner)


def after(x, *others):
    return lax.optimization_barrier((x,) + others)[0]


def ffn_kernel(part, *refs):
    h_ref, g_ref, *w_refs = refs[:6]
    dh_ref, ffn_ref, own0_ref, own1_ref, other_ref, w_ref = refs[6:]
    both = 2 * part
    q = w_refs[0].shape[1]
    cut = [slice(i * q, (i + 1) * q) for i in range(4)]
    for w, c in zip(w_refs, cut):
        w_ref[:, c] = w[...]
    h, g = h_ref[...], g_ref[...]
    gate_up = dot(w_ref[:both], h, 1, 1)
    d_hidden = dot(w_ref[both:], g, 1, 1)
    gate, up = gate_up[:part], gate_up[part:]
    sigma = 1.0 / (1.0 + jnp.exp(-gate))
    silu = gate * sigma
    hidden = (silu * up).astype(bf16)
    d_gate = (d_hidden * up * sigma * (1.0 + gate * (1.0 - sigma))).astype(bf16)
    d_up = (d_hidden * silu).astype(bf16)
    d_both = jnp.concatenate([d_gate, d_up], axis=0)
    dh_ref[...] = dot(d_both, w_ref[:both], 0, 0).astype(bf16)
    ffn_ref[...] = dot(hidden, w_ref[both:], 0, 0).astype(bf16)
    for rows, a, b in ((slice(0, both), d_both, h), (slice(both, 3 * part), hidden, g)):
        grad = dot(a, b, 1, 0)
        own0_ref[rows] = grad[:, cut[0]].astype(bf16)
        own1_ref[rows] = grad[:, cut[1]].astype(bf16)
        other_ref[rows] = grad[:, 2 * q :].astype(bf16)


def ffn_chunk(h, g, weights):
    tokens, D = h.shape
    n, q = weights[0].shape
    part = n // 3

    def kernel(*refs):
        ffn_kernel(part, *refs)

    return pl.pallas_call(
        kernel,
        out_shape=[
            jax.ShapeDtypeStruct((tokens, D), bf16),
            jax.ShapeDtypeStruct((tokens, D), bf16),
            jax.ShapeDtypeStruct((n, q), bf16),
            jax.ShapeDtypeStruct((n, q), bf16),
            jax.ShapeDtypeStruct((n, 2 * q), bf16),
        ],
        scratch_shapes=[pltpu.VMEM((n, D), bf16)],
        compiler_params=pltpu.CompilerParams(vmem_limit_bytes=58 * 1024 * 1024),
        cost_estimate=pl.CostEstimate(
            flops=20 * tokens * D * part, bytes_accessed=12 * n * q * 2, transcendentals=tokens * part
        ),
        interpret=INTERPRET,
    )(h, g, *weights)


def make_body(links):
    dp, T = links.dp, links.tensor

    def body(x_in, in_w, out_w, gate_w, up_w, down_w, conv_w, gain1, gain2, d_out):
        rows, D = x_in.shape
        block = D // dp
        half = D // 2
        chan = in_w.shape[2]
        C = chan * T
        part = gate_w.shape[1] // 2
        per_seq = LEN // rows
        me_dp = lax.axis_index("dp")
        me_t = lax.axis_index("tensor")
        me_x = (me_dp // 2) % 2
        core = me_dp % 2
        groups = dp // 2
        canonical = [
            [sum(((q >> links.bit(c, j)) & 1) << j for j in range(links.bits)) for q in range(groups)] for c in (0, 1)
        ]
        walked = [[order.index(p) for p in range(groups)] for order in canonical]

        def by_core(blocks, order):
            a, b = order
            return [blocks[i] if i == j else jnp.where(core == 0, blocks[i], blocks[j]) for i, j in zip(a, b)]

        def walk_start(own, got):
            x = own.astype(f32) + got.astype(f32)
            return by_core([x[i * block : (i + 1) * block] for i in range(groups)], walked)

        def walk_send(blocks, j):
            return send(jnp.concatenate(blocks[len(blocks) // 2 :], axis=0).astype(bf16), links.step(j))

        def walk_add(blocks, got):
            return [
                blocks[i] + got[i * block : (i + 1) * block].astype(f32) for i in range(len(blocks) // 2)
            ]

        def shift_back(k, x):
            return send(x.astype(bf16), [(b, a) for a, b in links.shift(k)])

        def swap(v):
            parts = [v[:, (p ^ 1) * block : ((p ^ 1) + 1) * block] for p in range(dp)]
            return jnp.concatenate(parts, axis=1)

        mine = me_dp ^ jnp.asarray([links.spread(p) for p in range(dp)], jnp.int32)
        source = (mine[:, None] * block + jnp.arange(block)[None, :]).reshape(D)
        place = (jnp.arange(D)[:, None] == source[None, :]).astype(bf16)

        def arrange(v):
            return dot(v, place, 1, 0).astype(bf16)

        def restore(v):
            return dot(v, place, 1, 1).astype(bf16)

        def restore_rows(v):
            return jnp.sum(
                jnp.where((mine[None, :] == jnp.arange(dp)[:, None])[:, :, None], v.reshape(1, dp, block), 0.0), axis=1
            ).reshape(D)

        in_own = in_w.reshape(block, 3 * chan)
        in_k = [in_own] + [send(in_own, links.shift(k)) for k in range(1, T)]
        stack = jnp.concatenate([w.reshape(2, part, block) for w in (gate_w.T, up_w.T, down_w)], axis=1)
        ffn_keep = jnp.where(me_x == 0, stack[0], stack[1])
        ffn_give = jnp.where(me_x == 0, stack[1], stack[0])
        ffn_own = jnp.concatenate([ffn_keep, send(ffn_give, links.flip(0))], axis=1)

        own = [ffn_own]
        near = [[] for _ in range(T)]

        def shift_chunk(*waits):
            if len(own) < T:
                own.append(send(after(own[-1], *waits), links.shift(1)))

        def exchange(k, *waits):
            if k < T:
                x = after(own[k], *waits)
                for j in range(1, links.bits):
                    got = send(x, links.flip(j))
                    near[k] = [x, got]
                    if j < links.bits - 1:
                        x = jnp.concatenate(near[k], axis=1)

        def walk_first(x):
            return [x, send(x, links.step(0))]

        def walk_rest(blocks, *waits):
            for j in range(1, links.bits):
                whole = jnp.concatenate(blocks, axis=0)
                if j == 1:
                    whole = after(whole, *waits)
                blocks = blocks + [send(whole, links.step(j))]
            return blocks

        def in_order(wholes):
            blocks = [w[i * block : (i + 1) * block] for w in wholes for i in range(w.shape[0] // block)]
            return jnp.concatenate(by_core(blocks, canonical), axis=0)

        in_cols = jnp.concatenate([w[:, i * chan : (i + 1) * chan] for i in range(3) for w in in_k], axis=1)
        x_arranged, cot16 = arrange(x_in), arrange(d_out)
        cot_swapped = swap(cot16)
        in_cols = after(in_cols, ffn_own, x_arranged, cot16, cot_swapped)
        in_first = walk_first(in_cols)
        out_own = after(out_w.T, in_cols)
        out_k = [out_own] + [send(out_own, links.shift(k)) for k in range(1, T)]
        out_cols = jnp.concatenate(out_k, axis=1)
        slot2 = [in_first[1], out_cols]
        in_walked = walk_rest(in_first, *slot2)
        out_first = walk_first(after(out_cols, *slot2))
        shift_chunk(*slot2)
        slot3 = [in_walked[-1], own[-1], out_first[1]]
        in0 = after(in_order(in_walked), *slot3)
        in1 = send(in0, links.cores())
        out_walked = walk_rest(out_first, *slot3)
        shift_chunk(*slot3)
        exchange(1, *slot3, out_walked[-1])
        out0 = in_order(out_walked)
        out1 = send(out0, links.cores())

        tokens = x_arranged.astype(f32)
        partner_cot = send(after(cot_swapped, *slot3, out_walked[-1]), links.flip(0))
        gains = arrange(jnp.stack([gain1, gain2])).astype(f32)
        gain_one, gain_two = gains[0], gains[1]
        turned = jnp.concatenate([conv_w, conv_w], axis=1)
        kernel = lax.dynamic_slice_in_dim(turned, me_t * chan, C, 1).astype(f32)

        def split(a, axis=1):
            return lax.slice_in_dim(a, 0, half, axis=axis), lax.slice_in_dim(a, half, D, axis=axis)

        normed_one, scale_one = norm_rows(tokens)
        first = (normed_one * gain_one).astype(bf16)
        f0, f1 = split(first)
        projected = dot(f0, in0, 1, 0) + dot(f1, in1, 1, 0)
        b_part, c_part, x_part = projected[:, :C], projected[:, C : 2 * C], projected[:, 2 * C :]
        mixed_in = b_part * x_part
        follows = [(links.at(d, t), links.at(d, t + 1)) for d, t in links.devices if (t + 1) % per_seq]
        no_rows = jnp.zeros((2, C), f32)
        before = send(jnp.roll(mixed_in[rows - 2 :], -chan, axis=1), follows) if follows else no_rows
        lead = jnp.concatenate([before, mixed_in[: rows - 1]], axis=0)
        back_one = lead[1:]
        back_two = lead[:rows]
        conv_out = kernel[2] * mixed_in + kernel[1] * back_one + kernel[0] * back_two
        branch = (c_part * conv_out).astype(bf16)
        slot4 = [out_walked[-1], own[-1], partner_cot] + near[1 % T]
        branch = after(branch, *slot4)
        exchange(2, branch)
        shift_chunk(branch)
        resid = tokens + jnp.concatenate([dot(branch, out0, 1, 1), dot(branch, out1, 1, 1)], axis=1)
        normed_two, scale_two = norm_rows(resid)
        second = (normed_two * gain_two).astype(bf16)
        cot_all = jnp.concatenate([partner_cot, cot16], axis=0)
        second_all = jnp.concatenate([send(swap(second), links.flip(0)), second], axis=0)

        def core_sum(own0, own1, other):
            got = send(other, links.cores())
            return [own0, got[:, : half // 2]], (own1.astype(f32) + got[:, half // 2 :].astype(f32)).astype(bf16)

        def group_sum(kept, sent):
            got = send(sent, links.flip(links.bits - 1))
            if links.bits == 2:
                return (lambda: sum(v.astype(f32) for v in kept + [got])), got
            x = sum(v.astype(f32) for v in kept + [got])
            for j in reversed(range(1, links.bits - 1)):
                n = x.shape[1] // 2
                got = send(x[:, n:].astype(bf16), links.flip(j))
                x = x[:, :n] + got.astype(f32)
            return (lambda: x), got

        def shift_sum(i, *waits):
            return shift_back(turn[i], after(grouped[i][0]().astype(bf16), *waits))

        def other_core(k):
            return near[k] + [send(x, links.cores()) for x in near[k]]

        turn = list(range(1, T)) + [0]
        d_h, ffn, sums, cored, grouped, shifted, weights = {}, {}, {}, {}, {}, {}, {}
        weights[turn[0]] = other_core(turn[0])
        slot = weights[turn[0]] + [x for k in turn[:2] for x in near[k]] + own
        for i, k in enumerate(turn):
            h_in = after(second_all, *slot)
            slot = []
            if i + 2 < T:
                exchange(turn[i + 2], h_in)
                slot += near[turn[i + 2]]
            if i + 1 < T:
                weights[turn[i + 1]] = other_core(turn[i + 1])
                slot += weights[turn[i + 1]]
            if i >= 1:
                cored[i - 1] = core_sum(*sums[i - 1])
                slot.append(cored[i - 1][1])
            if i >= 2:
                grouped[i - 2] = group_sum(cored[i - 2][0], after(cored[i - 2][1], h_in))
                slot.append(grouped[i - 2][1])
            if i >= 3:
                shifted[i - 3] = shift_sum(i - 3, h_in)
                slot.append(shifted[i - 3])
            d_h[k], ffn[k], *sums[i] = ffn_chunk(h_in, cot_all, weights[k])
            sums[i][2] = after(sums[i][2], *slot)

        def total(parts, rows_of):
            return sum(parts[k][rows_of].astype(f32) for k in turn)

        theirs, ours = slice(0, rows), slice(rows, 2 * rows)
        got = send(swap(total(d_h, theirs).astype(bf16)), links.flip(0))
        cored[T - 1] = core_sum(*sums[T - 1])
        if T > 1:
            grouped[T - 2] = group_sum(cored[T - 2][0], after(cored[T - 2][1], cored[T - 1][1]))
        if T > 2:
            shifted[T - 3] = shift_sum(T - 3, sums[T - 1][2])
        ffn_theirs = swap(total(ffn, theirs).astype(bf16))
        got = after(got, ffn_theirs, cored[T - 1][1], *[grouped[i][1] for i in grouped])
        d_second = total(d_h, ours) + got.astype(f32)
        ffn_sent = send(after(ffn_theirs, got), links.flip(0))
        grouped[T - 1] = group_sum(cored[T - 1][0], after(cored[T - 1][1], got))

        gain_two_part = jnp.sum(d_second * normed_two, axis=0)
        d_resid = cot16.astype(f32) + norm_back(d_second, normed_two, scale_two, gain_two)
        d_mixed = d_resid.astype(bf16)
        m0, m1 = split(d_mixed)
        d_branch = dot(m0, out0, 1, 0) + dot(m1, out1, 1, 0)
        d_conv = d_branch * c_part
        d_c = d_branch * conv_out
        leads = [(b, a) for a, b in follows]
        edge = send(jnp.roll(d_conv[:2], chan, axis=1), leads) if leads else no_rows
        d_c = d_c.astype(bf16)
        first_other = jnp.concatenate([dot(m1, branch, 0, 0), dot(f1, d_c, 0, 0)], axis=1).astype(bf16)
        first_got = send(first_other, links.cores())
        m0 = after(m0, grouped[T - 1][1])
        first_own = jnp.concatenate([dot(m0, branch, 0, 0), dot(f0, d_c, 0, 0)], axis=1).astype(bf16)
        edge = after(edge, first_own)
        if T > 1:
            shifted[T - 2] = shift_sum(T - 2, edge)
        first_blocks = walk_start(first_own, first_got)
        trail = jnp.concatenate([d_conv[1:], edge], axis=0)
        d_mixin = kernel[2] * d_conv + kernel[1] * trail[:rows] + kernel[0] * trail[1:]
        taps = [jnp.sum(d_conv * v, axis=0) for v in (back_two, back_one, mixed_in)]
        d_bx = jnp.concatenate([(d_mixin * v).astype(bf16) for v in (x_part, b_part)], axis=1)
        d_bx = after(d_bx, *first_blocks, *[shifted[i] for i in range(T - 2)])
        last_other = dot(f1, d_bx, 0, 0).astype(bf16)
        last_got = send(last_other, links.cores())
        last_own = dot(after(f0, last_other, ffn_sent), d_bx, 0, 0).astype(bf16)
        d_proj = jnp.concatenate([d_bx[:, :C], d_c, d_bx[:, C:]], axis=1)
        d_proj = after(d_proj, last_own)
        d_first = jnp.concatenate([dot(d_proj, in0, 1, 1), dot(d_proj, in1, 1, 1)], axis=1)
        *first_blocks, last_got, d_first = lax.optimization_barrier((*first_blocks, last_got, d_first))
        first_got = walk_send(first_blocks, links.bits - 1)
        last_blocks = walk_start(last_own, last_got)
        for j in reversed(range(links.bits)):
            last_got = walk_send(last_blocks, j)
            if j == links.bits - 1:
                tail = last_got
            first_blocks = walk_add(first_blocks, first_got)
            if j:
                first_got = walk_send(first_blocks, j - 1)
            last_blocks = walk_add(last_blocks, last_got)

        def pieces(v, parts):
            take = lambda i, k: v[:, i * C + k * chan : i * C + (k + 1) * chan]
            return [jnp.concatenate([take(i, k) for i in range(parts)], axis=1) for k in range(T)]

        def all_shifts(blocks):
            return blocks[0] + sum(shift_back(k, blocks[k]).astype(f32) for k in range(1, T))

        first_sum = all_shifts(pieces(first_blocks[0], 2))
        last_sum = all_shifts(pieces(last_blocks[0], 2))
        grad_out = first_sum[:, :chan]
        grad_in = jnp.stack([last_sum[:, :chan], first_sum[:, chan:], last_sum[:, chan:]], axis=1)

        gain_one_part = jnp.sum(d_first * normed_one, axis=0)
        d_x = restore((d_resid + norm_back(d_first, normed_one, scale_one, gain_one)).astype(bf16))
        block_out = restore((resid + total(ffn, ours) + after(ffn_sent, last_got).astype(f32)).astype(bf16))

        pieces_back = [after(shifted[i], tail) for i in shifted]
        ffn_sum = after(grouped[T - 1][0](), tail) + sum(v.astype(f32) for v in pieces_back)
        mine_sum = ffn_sum[:, :block]
        partner_sum = send(after(ffn_sum[:, block:].astype(bf16), last_got), links.flip(0)).astype(f32)
        low = jnp.where(me_x == 0, mine_sum, partner_sum)
        high = jnp.where(me_x == 0, partner_sum, mine_sum)
        grads = [
            jnp.concatenate([low[i * part : (i + 1) * part], high[i * part : (i + 1) * part]], axis=0) for i in range(3)
        ]

        taps = jnp.stack(taps)
        taps = lax.dynamic_slice_in_dim(jnp.concatenate([taps, taps], axis=1), C - me_t * chan, C, 1)
        small = jnp.concatenate([taps, restore_rows(gain_one_part)[None], restore_rows(gain_two_part)[None]], axis=0)
        small = small + send(small, links.cores())
        small = after(small, tail)
        for j in range(links.bits):
            small = small + send(small, links.flip(j))
        k = 1
        while k < T:
            small = small + send(small, links.pairs(lambda d, t: (d, t ^ k)))
            k *= 2
        return (
            block_out,
            d_x,
            grad_in,
            grad_out.T,
            grads[0].T,
            grads[1].T,
            grads[2],
            small[:3],
            small[3],
            small[4],
        )

    return body


def solution(mesh):
    links = Links(mesh.shape["dp"], mesh.shape["tensor"])
    in_specs = (
        P(("dp", "tensor"), None),
        P("dp", None, "tensor"),
        P("tensor", "dp"),
        P("dp", "tensor"),
        P("dp", "tensor"),
        P("tensor", "dp"),
        P(),
        P(),
        P(),
        P(("dp", "tensor"), None),
    )
    out_specs = (
        P(("dp", "tensor"), None),
        P(("dp", "tensor"), None),
        P("dp", None, "tensor"),
        P("tensor", "dp"),
        P("dp", "tensor"),
        P("dp", "tensor"),
        P("tensor", "dp"),
        P(),
        P(),
        P(),
    )
    return jax.shard_map(
        make_body(links), mesh=mesh, in_specs=in_specs, out_specs=out_specs, check_vma=False
    )
```
